128 devices in a mesh: seq: 16 (over z, x), fsdp: 8 (over y, core).
Axes of the slice: x: 4, y: 4, z: 4, core: 2. Of those that a mesh axis runs over, the one named last changes fastest.
Arguments:
- inputs: bfloat16 [2048, 2304], P('seq'), may hold values from -6.5 to 6.5
- d_out: bfloat16 [2048, 4096], P('seq', 'fsdp'), may hold values from -6 to 6
- w_query: bfloat16 [2304, 4096], P('seq', 'fsdp'), may hold values from -0.125 to 0.125
- w_key: bfloat16 [2304, 4096], P('seq', 'fsdp'), may hold values from -0.125 to 0.125
- w_value: bfloat16 [2304, 4096], P('seq', 'fsdp'), may hold values from -0.125 to 0.125
- w_beta: bfloat16 [2304, 32], P('seq', 'fsdp'), may hold values from -1 to 1
- w_gate_down: bfloat16 [2304, 128], P('seq'), may hold values from -0.125 to 0.125
- w_gate_up: bfloat16 [128, 4096], P(None, 'fsdp'), may hold values from -0.5 to 0.5
- conv_weight: float32 [3, 4, 4096], P(None, None, 'fsdp'), may hold values from -3 to 3
- decay_rate: float32 [4096], P('fsdp'), may hold values from 0 to 0.1
Outputs:
- grad_input: bfloat16 [2048, 2304], P(('seq', 'fsdp'))
- grad_w_query: float32 [2304, 4096], P('seq', 'fsdp')
- grad_w_key: float32 [2304, 4096], P('seq', 'fsdp')
- grad_w_value: float32 [2304, 4096], P('seq', 'fsdp')
- grad_w_beta: float32 [2304, 32], P('seq', 'fsdp')
- grad_w_gate_down: float32 [2304, 128], P('seq')
- grad_w_gate_up: float32 [128, 4096], P(None, 'fsdp')
- grad_conv: float32 [3, 4, 4096], P(None, None, 'fsdp')
- grad_decay: float32 [4096], P('fsdp')
The draws below stay inside these ranges and needn't reach their ends.
All inputs are finite; a program needn't handle non-finite values.
Results may differ from the reference program's by a relative error of at most 0.017.
Values may be sent and summed in bfloat16 or wider, within the bound.
No kernel may reach another device: no remote copies, remote signals or barrier semaphores. Data moves between devices by JAX's collectives and lax.ppermute only.
A program may use at most 128 MiB of HBM per device.

```python
import jax
import jax.numpy as jnp
from jax import lax

D = 2304
HEADS = 32
DK = 128
GATE_RANK = 128
CONV = 4
SPAN = 64
TOKENS = 2048


def shared_parts(key):
    base = jax.random.fold_in(key, 7)
    signs = jax.random.randint(jax.random.fold_in(base, 1), (D,), 0, 2).astype(jnp.float32)
    common = signs - 0.5
    order = jax.random.permutation(jax.random.fold_in(base, 2), HEADS)
    chosen = order < HEADS // 2
    depth = jax.random.uniform(jax.random.fold_in(base, 3), (HEADS,), jnp.float32, -6.0, -5.0)
    shift = jnp.where(chosen, depth, jnp.zeros_like(depth))
    return (common, shift)


def draw_inputs(key, part):
    common, shift = shared_parts(key)
    noise = jax.random.truncated_normal(jax.random.fold_in(key, 11), -6.0, 6.0, (TOKENS, D), jnp.float32)
    return (noise + common[None, :]).astype(jnp.bfloat16)


def draw_w_beta(key, part):
    common, shift = shared_parts(key)
    noise = jax.random.truncated_normal(jax.random.fold_in(key, 12), -6.0, 6.0, (D, HEADS), jnp.float32) * D ** (-0.5)
    steer = common[:, None] * shift[None, :] * (4.0 / D)
    return (noise + steer).astype(jnp.bfloat16)


def draw_decay_rate(key, part):
    base = jax.random.fold_in(key, 13)
    width = HEADS * DK
    picks = jax.random.randint(jax.random.fold_in(base, 1), (width,), 0, 2) == 1
    slow_log = jax.random.uniform(jax.random.fold_in(base, 2), (width,), jnp.float32, jnp.log(0.2 / TOKENS), jnp.log(2.0 / TOKENS))
    fast_log = jax.random.uniform(jax.random.fold_in(base, 3), (width,), jnp.float32, jnp.log(4.0 / TOKENS), jnp.log(0.1))
    return jnp.exp(jnp.where(picks, slow_log, fast_log)).astype(jnp.float32)


def shard_levels(own_key, extent, cuts, least, top_value):
    level, own = 1.0, jax.random.fold_in(own_key, 6)
    for dim, blocks in cuts:
        draws = jnp.exp(jax.random.uniform(jax.random.fold_in(own, dim), (blocks,), jnp.float32, least / len(cuts), top_value / len(cuts)))
        level = level * jnp.repeat(draws, extent[dim] // blocks).reshape([-1 if axis == dim else 1 for axis in range(len(extent))])
    return level


def scatter_about(stream_key, extent, spread, most, split=(), kind=jnp.bfloat16):
    entries = spread * jax.random.normal(stream_key, extent, jnp.float32)
    if split:
        entries = entries * shard_levels(stream_key, extent, split, -0.22, 0.18)
    return jnp.clip(entries, -most, most).astype(kind)


def setup_inputs(seed: int = 0) -> dict:
    keys = jax.random.split(jax.random.key(seed), 11)
    inputs = draw_inputs(jax.random.fold_in(keys[10], 71), 0)
    d_out = scatter_about(keys[1], (TOKENS, HEADS * DK), 1.0, 6.0, ((0, 16), (1, 8)))
    w_query = scatter_about(keys[2], (D, HEADS * DK), D ** -0.5, 0.125, ((0, 16), (1, 8)))
    w_key = scatter_about(keys[3], (D, HEADS * DK), D ** -0.5, 0.125, ((0, 16), (1, 8)))
    w_value = scatter_about(keys[4], (D, HEADS * DK), D ** -0.5, 0.125, ((0, 16), (1, 8)))
    w_beta = draw_w_beta(jax.random.fold_in(keys[10], 71), 0)
    w_gate_down = scatter_about(keys[6], (D, GATE_RANK), D ** -0.5, 0.125, ((0, 16),))
    w_gate_up = scatter_about(keys[7], (GATE_RANK, HEADS * DK), GATE_RANK ** -0.5, 0.5, ((1, 8),))
    conv_weight = scatter_about(keys[8], (3, CONV, HEADS * DK), 0.5, 3.0, ((2, 8),), jnp.float32)
    decay_rate = draw_decay_rate(jax.random.fold_in(keys[10], 71), 0)
    return {"inputs": inputs, "d_out": d_out, "w_query": w_query, "w_key": w_key, "w_value": w_value, "w_beta": w_beta, "w_gate_down": w_gate_down, "w_gate_up": w_gate_up, "conv_weight": conv_weight, "decay_rate": decay_rate}


highest = lax.Precision.HIGHEST

def span_step(carried, pieces):
    queries, key_rows, value_rows, strength, log_decay = pieces
    cumulative = jnp.cumsum(log_decay, axis=1)
    grown_keys = key_rows * jnp.exp(cumulative)
    shrunk = key_rows * jnp.exp(-cumulative)
    lifted = queries * jnp.exp(cumulative)
    span_len = key_rows.shape[1]
    row_ids = lax.broadcasted_iota(jnp.int32, (span_len, span_len), 0)
    col_ids = lax.broadcasted_iota(jnp.int32, (span_len, span_len), 1)
    strict = (row_ids > col_ids).astype(jnp.float32)
    causal = (row_ids >= col_ids).astype(jnp.float32)
    diagonal = (row_ids == col_ids).astype(jnp.float32)
    mixing = jnp.einsum('hck,hdk->hcd', grown_keys, shrunk, precision=highest)
    system = diagonal + strength[:, :, None] * mixing * strict
    targets = strength[:, :, None] * (value_rows - jnp.einsum('hck,hkw->hcw', grown_keys, carried, precision=highest))
    deltas = lax.linalg.triangular_solve(system, targets, left_side=True, lower=True, unit_diagonal=True)
    scores = jnp.einsum('hck,hdk->hcd', lifted, shrunk, precision=highest) * causal
    outputs = jnp.einsum('hck,hkw->hcw', lifted, carried, precision=highest) + jnp.einsum('hcd,hdw->hcw', scores, deltas, precision=highest)
    final_decay = cumulative[:, -1:, :]
    tail_keys = key_rows * jnp.exp(final_decay - cumulative)
    new_state = jnp.exp(final_decay)[:, 0, :, None] * carried + jnp.einsum('hck,hcw->hkw', tail_keys, deltas, precision=highest)
    return (new_state, outputs)

def run_block(carried, queries, key_rows, value_rows, strength, log_decay, span_len):
    head_count = key_rows.shape[0]
    length = key_rows.shape[1]
    spans = length // span_len

    def regroup(values_in):
        return jnp.moveaxis(values_in.reshape((head_count, spans, span_len) + values_in.shape[2:]), 1, 0)
    final, outputs = lax.scan(span_step, carried, (regroup(queries), regroup(key_rows), regroup(value_rows), regroup(strength), regroup(log_decay)))
    outputs = jnp.moveaxis(outputs, 0, 1).reshape(head_count, length, value_rows.shape[2])
    return (outputs, final)

def features(projected, rim_rows, conv_weight, decay_rate, gate_pre, beta_lin):
    length = projected.shape[1]
    conv_taps = conv_weight.shape[1]
    padded = jnp.concatenate([rim_rows, projected], axis=1)
    mixture = conv_weight[:, 0, None, :] * padded[:, 0:length, :]
    for offset in range(1, conv_taps):
        mixture = mixture + conv_weight[:, offset, None, :] * padded[:, offset:offset + length, :]
    active = jax.nn.silu(mixture)
    head_count = active.shape[2] // DK
    per_head = jnp.transpose(active.reshape(3, length, head_count, DK), (0, 2, 1, 3))
    queries = per_head[0] / jnp.sqrt(lax.optimization_barrier(jnp.sum(per_head[0] * per_head[0], axis=-1, keepdims=True)) + 1e-06) * DK ** (-0.5)
    key_rows = per_head[1] / jnp.sqrt(lax.optimization_barrier(jnp.sum(per_head[1] * per_head[1], axis=-1, keepdims=True)) + 1e-06)
    value_rows = per_head[2]
    strength = jnp.transpose(jax.nn.sigmoid(beta_lin))
    log_decay = -decay_rate * jax.nn.sigmoid(gate_pre)
    log_decay = jnp.transpose(log_decay.reshape(length, head_count, DK), (1, 0, 2))
    return (queries, key_rows, value_rows, strength, log_decay)

def reference(inputs, d_out, w_query, w_key, w_value, w_beta, w_gate_down, w_gate_up, conv_weight, decay_rate):
    projected = jnp.stack([jnp.dot(inputs.astype(jnp.float32), matrix.astype(jnp.float32), preferred_element_type=jnp.float32) for matrix in (w_query, w_key, w_value)]).astype(jnp.bfloat16)
    beta_lin = jnp.dot(inputs.astype(jnp.float32), w_beta.astype(jnp.float32), preferred_element_type=jnp.float32)
    low_rank = jnp.dot(inputs.astype(jnp.float32), w_gate_down.astype(jnp.float32), preferred_element_type=jnp.float32).astype(jnp.bfloat16)
    gate_pre = jnp.dot(low_rank.astype(jnp.float32), w_gate_up.astype(jnp.float32), preferred_element_type=jnp.float32)
    columns = w_query.shape[1]
    rim_rows = jnp.zeros((3, CONV - 1, columns), jnp.float32)
    head_inputs, input_pull = jax.vjp(features, projected.astype(jnp.float32), rim_rows, conv_weight, decay_rate, gate_pre, beta_lin)
    zero_state = jnp.zeros((HEADS, DK, DK), jnp.float32)

    def outputs_of(five):
        return run_block(zero_state, five[0], five[1], five[2], five[3], five[4], SPAN)[0]
    unused, block_pull = jax.vjp(outputs_of, head_inputs)
    cotangent = jnp.transpose(d_out.astype(jnp.float32).reshape(TOKENS, HEADS, DK), (1, 0, 2))
    head_grads, = block_pull(cotangent)
    proj_grads, rim_cotangent, grad_conv, grad_decay, gate_grads, beta_grads = input_pull(head_grads)
    proj_grads = proj_grads.astype(jnp.bfloat16)
    gate_grads = gate_grads.astype(jnp.bfloat16)
    beta_grads = beta_grads.astype(jnp.bfloat16)
    low_grads = jnp.dot(gate_grads.astype(jnp.float32), w_gate_up.T.astype(jnp.float32), preferred_element_type=jnp.float32).astype(jnp.bfloat16)
    grad_w_gate_up = jnp.dot(low_rank.T.astype(jnp.float32), gate_grads.astype(jnp.float32), preferred_element_type=jnp.float32)
    grad_w_query = jnp.dot(inputs.T.astype(jnp.float32), proj_grads[0].astype(jnp.float32), preferred_element_type=jnp.float32)
    grad_w_key = jnp.dot(inputs.T.astype(jnp.float32), proj_grads[1].astype(jnp.float32), preferred_element_type=jnp.float32)
    grad_w_value = jnp.dot(inputs.T.astype(jnp.float32), proj_grads[2].astype(jnp.float32), preferred_element_type=jnp.float32)
    grad_w_beta = jnp.dot(inputs.T.astype(jnp.float32), beta_grads.astype(jnp.float32), preferred_element_type=jnp.float32)
    grad_w_gate_down = jnp.dot(inputs.T.astype(jnp.float32), low_grads.astype(jnp.float32), preferred_element_type=jnp.float32)
    grad_input = jnp.dot(proj_grads[0].astype(jnp.float32), w_query.T.astype(jnp.float32), preferred_element_type=jnp.float32)
    grad_input = grad_input + jnp.dot(proj_grads[1].astype(jnp.float32), w_key.T.astype(jnp.float32), preferred_element_type=jnp.float32)
    grad_input = grad_input + jnp.dot(proj_grads[2].astype(jnp.float32), w_value.T.astype(jnp.float32), preferred_element_type=jnp.float32)
    grad_input = grad_input + jnp.dot(beta_grads.astype(jnp.float32), w_beta.T.astype(jnp.float32), preferred_element_type=jnp.float32)
    grad_input = grad_input + jnp.dot(low_grads.astype(jnp.float32), w_gate_down.T.astype(jnp.float32), preferred_element_type=jnp.float32)
    return (grad_input.astype(jnp.bfloat16), grad_w_query, grad_w_key, grad_w_value, grad_w_beta, grad_w_gate_down, grad_w_gate_up, grad_conv, grad_decay)
```

```python
import jax
import jax.numpy as jnp
from jax import lax
from jax.experimental import pallas as pl
from jax.experimental.pallas import tpu as pltpu
from jax.sharding import Mesh, PartitionSpec as P

DK = 128
CONV = 4
RIM = 16
SPAN = 128
F32 = jnp.float32
BF16 = jnp.bfloat16


def parts_of(x, wide=True):
    high = x.astype(BF16)
    if not wide:
        return (high, None)
    return (high, (x - high.astype(F32)).astype(BF16))


def product(a, b, dims=(1, 0)):
    def one(x, y):
        return lax.dot_general(
            x, y, (((dims[0],), (dims[1],)), ((), ())), preferred_element_type=F32
        )

    out = one(a[0], b[0])
    if a[1] is not None:
        out = out + one(a[1], b[0])
    if b[1] is not None:
        out = out + one(a[0], b[1])
    return out


def both(a, b, axis):
    return tuple(jnp.concatenate([x, y], axis=axis) for x, y in zip(a, b))


def flip(a):
    return tuple(None if x is None else x.T for x in a)


def sigmoid(x):
    return 1.0 / (1.0 + jnp.exp(-x))


def indices():
    rows = lax.broadcasted_iota(jnp.int32, (SPAN, SPAN), 0)
    cols = lax.broadcasted_iota(jnp.int32, (SPAN, SPAN), 1)
    return rows, cols


def unit_inverses(lowers, rows, cols):
    def block(size):
        near = (rows // (2 * size)) == (cols // (2 * size))
        return near & ((rows // size) % 2 == 1) & ((cols // size) % 2 == 0)

    first = block(1)
    eye = jnp.where(rows == cols, 1.0, 0.0)
    inverses = [eye - jnp.where(first, lower, 0.0) for lower in lowers]
    size = 2
    while size < SPAN:
        here = block(size)
        held = [parts_of(x) for x in inverses]
        corners = [parts_of(jnp.where(here, lower, 0.0)) for lower in lowers]
        corners = [parts_of(product(x, y)) for x, y in zip(corners, held)]
        inverses = [x - product(y, w) for x, y, w in zip(inverses, held, corners)]
        size *= 2
    return inverses


def mixed(taps_ref, pad_ref, kind, start):
    total = None
    for tap in range(CONV):
        first = RIM - (CONV - 1) + tap + start
        term = taps_ref[kind * CONV + tap : kind * CONV + tap + 1, :] * pad_ref[
            kind, first : first + SPAN, :
        ]
        total = term if total is None else total + term
    return total


def lengths(active):
    return lax.rsqrt(jnp.sum(active * active, axis=1, keepdims=True) + 1e-06)


def fill_pad(proj_ref, pad_ref):
    for kind in range(3):
        pad_ref[kind] = proj_ref[:, kind * DK : (kind + 1) * DK].astype(F32)


def gates(proj_ref, up_ref, rate_ref, start):
    low = proj_ref[RIM + start : RIM + start + SPAN, 3 * DK :]
    gate = sigmoid(jnp.dot(low, up_ref[...], preferred_element_type=F32))
    return gate


def ahead_body(
    proj_ref, up_ref, taps_ref, rate_ref, beta_ref, cot_ref,
    pay_ref, cum_ref, inv_ref, uw_ref, score_ref, mix_ref, back_ref, map_ref, add_ref, give_ref,
    pad_ref,
):
    rows, cols = indices()
    summing = (jnp.where(rows >= cols, 1.0, 0.0).astype(BF16), None)
    fill_pad(proj_ref, pad_ref)
    spans = beta_ref.shape[0] // SPAN
    ats = [slice(n * SPAN, (n + 1) * SPAN) for n in range(spans)]
    values, strengths, growns, lifteds, tails, lasts = [], [], [], [], [], []
    mixes, scores = [], []
    for n, at in enumerate(ats):
        act = [jax.nn.silu(mixed(taps_ref, pad_ref, kind, n * SPAN)) for kind in range(3)]
        queries = act[0] * lengths(act[0]) * DK ** (-0.5)
        keys = act[1] * lengths(act[1])
        decay = -rate_ref[...] * gates(proj_ref, up_ref, rate_ref, n * SPAN)
        cum = product(summing, parts_of(decay))
        grow = jnp.exp(cum)
        shrunk = keys * jnp.exp(-cum)
        values.append(act[2])
        strengths.append(sigmoid(beta_ref[at, :]))
        growns.append(keys * grow)
        lifteds.append(queries * grow)
        lasts.append(grow[SPAN - 1 : SPAN, :])
        tails.append(shrunk * lasts[n])
        pairs = product(
            both(parts_of(growns[n]), parts_of(lifteds[n]), 0), parts_of(shrunk), (1, 1)
        )
        mixes.append(jnp.where(rows > cols, pairs[:SPAN], 0.0))
        scores.append(jnp.where(rows >= cols, pairs[SPAN:], 0.0))
        cum_ref[at, :] = cum
        mix_ref[at, :] = mixes[n]
        score_ref[at, :] = scores[n]
    inverses = unit_inverses([b * m for b, m in zip(strengths, mixes)], rows, cols)
    uws = [
        product(parts_of(inverses[n]), parts_of(jnp.concatenate(
            [strengths[n] * values[n], strengths[n] * growns[n]], axis=1
        )))
        for n in range(spans)
    ]
    turned = [product(parts_of(tails[n].T), parts_of(uws[n])) for n in range(spans)]
    cots = [(cot_ref[at, :], None) for at in ats]
    backs = [product(parts_of(scores[n].T), cots[n]) for n in range(spans)]
    gives = [
        product(parts_of(lifteds[n].T), cots[n])
        - product(parts_of(uws[n][:, DK:].T), parts_of(backs[n]))
        for n in range(spans)
    ]
    maps = [jnp.where(rows == cols, lasts[n], 0.0) - turned[n][:, DK:] for n in range(spans)]
    adds = [turned[n][:, :DK] for n in range(spans)]
    for n, at in enumerate(ats):
        inv_ref[at, :] = inverses[n]
        uw_ref[at, :] = uws[n]
        back_ref[at, :] = backs[n]
        map_ref[at, :] = maps[n]
        add_ref[at, :] = adds[n]
        give_ref[at, :] = gives[n]
    joined = jnp.concatenate([maps[0], adds[0]], axis=1)
    for n in range(1, spans):
        joined = product(parts_of(maps[n]), parts_of(joined))
        joined = joined + jnp.concatenate([jnp.zeros_like(adds[n]), adds[n]], axis=1)
    given = gives[spans - 1]
    for n in range(spans - 2, -1, -1):
        given = product(parts_of(maps[n].T), parts_of(given)) + gives[n]
    pay_ref[0:DK, :] = joined[:, :DK].astype(BF16)
    pay_ref[DK : 2 * DK, :] = joined[:, DK:].astype(BF16)
    pay_ref[2 * DK :, :] = given.astype(BF16)


def after_body(
    place_ref, *refs
):
    after_inner(place_ref[0], refs[:-20], *refs[-20:])


def after_inner(
    place, peer_refs, proj_ref, up_ref, taps_ref, rate_ref, beta_ref, cot_ref,
    cum_ref, inv_ref, uw_ref, score_ref, mix_ref, back_ref, map_ref, add_ref, give_ref,
    grads_ref, bgrad_ref, small_ref,
    pad_ref, mgrad_ref,
):
    rows, cols = indices()
    summing = (jnp.where(rows <= cols, 1.0, 0.0).astype(BF16), None)
    fill_pad(proj_ref, pad_ref)
    spans = beta_ref.shape[0] // SPAN
    length = spans * SPAN
    peers = len(peer_refs)

    state = jnp.zeros((DK, DK), F32)
    leave = jnp.zeros((DK, DK), F32)
    for d in range(peers, 0, -1):
        ref = peer_refs[d - 1]
        new = ref[DK : 2 * DK, :].astype(F32)
        if d < peers:
            new = new + product((ref[0:DK, :], None), parts_of(state))
        state = jnp.where(d <= place, new, state)
        ref = peer_refs[peers - d]
        new = ref[2 * DK :, :].astype(F32)
        if d < peers:
            new = new + product((ref[0:DK, :].astype(F32).T.astype(BF16), None), parts_of(leave))
        leave = jnp.where(place + d <= peers, new, leave)
    states = [state]
    for n in range(spans - 1):
        at = slice(n * SPAN, (n + 1) * SPAN)
        states.append(product(parts_of(map_ref[at, :]), parts_of(states[n])) + add_ref[at, :])
    leaves = [None] * spans
    leaves[spans - 1] = leave
    for n in range(spans - 1, 0, -1):
        at = slice(n * SPAN, (n + 1) * SPAN)
        leaves[n - 1] = (
            product(parts_of(map_ref[at, :].T), parts_of(leaves[n])) + give_ref[at, :]
        )

    for kind in range(3):
        mgrad_ref[kind, 0:RIM, :] = jnp.zeros((RIM, DK), F32)
        mgrad_ref[kind, RIM + length :, :] = jnp.zeros((8, DK), F32)
    tap_sums = [jnp.zeros((1, DK), F32) for _ in range(3 * CONV)]
    rate_sum = jnp.zeros((1, DK), F32)
    up_sum = jnp.zeros((DK, DK), F32)
    grads_ref[0:RIM, 3 * DK :] = jnp.zeros((RIM, DK), BF16)
    for n in range(spans):
        at = slice(n * SPAN, (n + 1) * SPAN)
        mixture = [mixed(taps_ref, pad_ref, kind, n * SPAN) for kind in range(3)]
        gated = [sigmoid(m) for m in mixture]
        act = [m * s for m, s in zip(mixture, gated)]
        scale_q = lengths(act[0])
        scale_k = lengths(act[1])
        unit_q = act[0] * scale_q
        queries = unit_q * DK ** (-0.5)
        keys = act[1] * scale_k
        values = act[2]
        strength = sigmoid(beta_ref[at, :])
        gate = gates(proj_ref, up_ref, rate_ref, n * SPAN)
        cum = cum_ref[at, :]
        grow = jnp.exp(cum)
        fall = jnp.exp(-cum)
        shrunk = keys * fall
        grown = keys * grow
        lifted = queries * grow
        last = grow[SPAN - 1 : SPAN, :]
        tail = shrunk * last
        mix = mix_ref[at, :]
        uw = uw_ref[at, :]
        p_state = parts_of(states[n])
        p_leave = parts_of(leaves[n])
        read = product(both(parts_of(uw[:, DK:]), parts_of(grown), 0), p_state)
        delta = uw[:, :DK] - read[:SPAN]
        rest = values - read[SPAN:]
        p_delta = parts_of(delta)
        cot = (cot_ref[at, :], None)
        ddelta = back_ref[at, :] + product(parts_of(tail), p_leave)
        y = product(parts_of(inv_ref[at, :].T), parts_of(ddelta))
        z = strength * y
        e = jnp.where(rows > cols, product(parts_of(y), p_delta, (1, 1)), 0.0)
        dscore = jnp.where(rows >= cols, product(cot, p_delta, (1, 1)), 0.0)
        dmix = -strength * e
        dstrength = jnp.sum(y * rest - e * mix, axis=1, keepdims=True)
        p_dscore = parts_of(dscore)
        p_dmix = parts_of(dmix)
        through = product(
            both((cot[0], jnp.zeros_like(cot[0])), parts_of(-z), 0), p_state, (1, 1)
        )
        crossed = product(both(p_dscore, p_dmix, 0), parts_of(shrunk))
        dlifted = through[:SPAN] + crossed[:SPAN]
        dgrown = through[SPAN:] + crossed[SPAN:]
        dshrunk = product(parts_of(dmix.T), parts_of(grown)) + product(
            parts_of(dscore.T), parts_of(lifted)
        )
        dtail = product(p_delta, p_leave, (1, 1))
        dquery = dlifted * grow
        dkey = dgrown * grow + (dshrunk + dtail * last) * fall
        tails = dtail * tail
        dcum = dlifted * lifted + dgrown * grown - dshrunk * shrunk - tails
        carried = jnp.sum((states[n] * leaves[n]).T, axis=0, keepdims=True) * last
        dlast = jnp.sum(tails, axis=0, keepdims=True) + carried
        ddecay = product(summing, parts_of(dcum)) + dlast
        rate_sum = rate_sum - jnp.sum(ddecay * gate, axis=0, keepdims=True)
        ggrad = (-ddecay * rate_ref[...] * gate * (1.0 - gate)).astype(BF16)
        low = proj_ref[RIM + n * SPAN : RIM + (n + 1) * SPAN, 3 * DK :]
        up_sum = up_sum + jnp.dot(
            low.astype(F32).T.astype(BF16), ggrad, preferred_element_type=F32
        )
        grads_ref[RIM + n * SPAN : RIM + (n + 1) * SPAN, 3 * DK :] = lax.dot_general(
            ggrad, up_ref[...], (((1,), (1,)), ((), ())), preferred_element_type=F32
        ).astype(BF16)
        bgrad_ref[at, :] = dstrength * strength * (1.0 - strength)
        dq = dquery * DK ** (-0.5)
        dact = [
            scale_q * (dq - unit_q * jnp.sum(unit_q * dq, axis=1, keepdims=True)),
            scale_k * (dkey - keys * jnp.sum(keys * dkey, axis=1, keepdims=True)),
            z,
        ]
        for kind in range(3):
            s = gated[kind]
            dm = dact[kind] * (s * (1.0 + mixture[kind] * (1.0 - s)))
            mgrad_ref[kind, RIM + n * SPAN : RIM + (n + 1) * SPAN, :] = dm
            for tap in range(CONV):
                first = RIM - (CONV - 1) + tap + n * SPAN
                tap_sums[kind * CONV + tap] = tap_sums[kind * CONV + tap] + jnp.sum(
                    dm * pad_ref[kind, first : first + SPAN, :], axis=0, keepdims=True
                )
    for kind in range(3):
        for start in [0] + [RIM + n * SPAN for n in range(spans)]:
            size = RIM if start == 0 else SPAN
            total = None
            for tap in range(CONV):
                first = start + CONV - 1 - tap
                term = (
                    taps_ref[kind * CONV + tap : kind * CONV + tap + 1, :]
                    * mgrad_ref[kind, first : first + size, :]
                )
                total = term if total is None else total + term
            grads_ref[start : start + size, kind * DK : (kind + 1) * DK] = total.astype(BF16)
    small_ref[0:DK, :] = up_sum.astype(BF16)
    small_ref[DK:, :] = jnp.concatenate(
        tap_sums + [rate_sum, jnp.zeros((3, DK), F32)], axis=0
    ).astype(BF16)


def shifted(block, axis, distance):
    size = lax.axis_size(axis)
    return lax.ppermute(block, axis, [(i, (i + distance) % size) for i in range(size)])


def placed(blocks, axis):
    size, place = lax.axis_size(axis), lax.axis_index(axis)
    out = jnp.zeros((size,) + blocks[0].shape, blocks[0].dtype)
    for k, block in enumerate(blocks):
        out = lax.dynamic_update_slice_in_dim(out, block[None], (place - k) % size, axis=0)
    return out


def ring_gather(block, axis):
    half = block.shape[0] // 2
    behind = shifted(block, axis, 1)
    ahead = shifted(block, axis, -1)
    far = jnp.concatenate(
        [shifted(behind[:half], axis, 1), shifted(ahead[half:], axis, -1)], axis=0
    )
    return placed([block, behind, far, ahead], axis)


def ring_scatter(blocks, axis):
    total = blocks[0].astype(F32)
    for d in range(1, len(blocks)):
        total = total + shifted(blocks[d], axis, d).astype(F32)
    return total


def ordered_sum(blocks, axis):
    moved = [blocks[0]] + [shifted(blocks[d], axis, d) for d in range(1, len(blocks))]
    return jnp.sum(placed(moved, axis).astype(F32), axis=0)


def on_device(
    inputs, d_out, w_query, w_key, w_value, w_beta, w_gate_down, w_gate_up, conv_weight, decay_rate
):
    toks = inputs.shape[0]
    rows_own = w_query.shape[0]
    width = inputs.shape[1]
    xs, zs, ys, cs = (lax.axis_size(name) for name in ("x", "z", "y", "c"))
    head, quarter, row, core = (lax.axis_index(name) for name in ("x", "z", "y", "c"))
    length = xs * toks

    def heads(array):
        return jnp.transpose(array.reshape(array.shape[0], xs, DK), (1, 0, 2))

    def own_head(array):
        return lax.dynamic_slice_in_dim(array, head * DK, DK, axis=array.ndim - 1)

    down = jnp.broadcast_to(w_gate_down[None], (xs, rows_own, DK))
    send = jnp.concatenate([heads(w_query), heads(w_key), heads(w_value), down], axis=2)
    got = lax.all_to_all(send, "x", 0, 0, tiled=True).reshape(xs * rows_own, 4 * DK)
    weights = ring_gather(got, "z").reshape(width, 4 * DK)

    half = toks // cs
    mine = lax.dynamic_slice_in_dim(inputs, core * half, half, axis=0)
    mine = ring_gather(mine, "x")
    theirs = shifted(mine, "c", 1)
    tokens = jnp.zeros((xs, cs, half, width), BF16)
    tokens = lax.dynamic_update_slice_in_dim(tokens, mine[:, None], core, axis=1)
    tokens = lax.dynamic_update_slice_in_dim(tokens, theirs[:, None], 1 - core, axis=1)
    tokens = tokens.reshape(length, width)

    cot = lax.all_to_all(heads(d_out), "x", 0, 0, tiled=True).reshape(length, DK)
    beta_send = jnp.broadcast_to(jnp.transpose(w_beta)[None], (zs, xs, rows_own)).reshape(
        zs * xs, rows_own
    )
    w_strength = lax.all_to_all(beta_send, ("z", "x"), 0, 0, tiled=True).reshape(1, width)
    rim = lax.ppermute(tokens[length - RIM :], "z", [(i, i + 1) for i in range(zs - 1)])
    rim = jnp.where(
        lax.broadcasted_iota(jnp.int32, rim.shape, 0) >= RIM - (CONV - 1), rim, jnp.zeros_like(rim)
    )
    reach = jnp.concatenate([rim, tokens], axis=0)
    up = own_head(w_gate_up)
    taps = own_head(conv_weight).reshape(3 * CONV, DK)
    rate = own_head(decay_rate[None])
    beta_lin = lax.dot_general(
        tokens, w_strength, (((1,), (1,)), ((), ())), preferred_element_type=F32
    )
    proj = jnp.dot(reach, weights, preferred_element_type=F32).astype(BF16)

    square = jax.ShapeDtypeStruct((length, DK), F32)
    pay, cum, inv, uw, score, mix, back, maps, adds, gives = pl.pallas_call(
        ahead_body,
        out_shape=(
            jax.ShapeDtypeStruct((3 * DK, DK), BF16),
            square,
            square,
            jax.ShapeDtypeStruct((length, 2 * DK), F32),
            square,
            square,
            square,
            square,
            square,
            square,
        ),
        scratch_shapes=[pltpu.VMEM((3, RIM + length, DK), F32)],
        name="ahead",
    )(proj, up, taps, rate, beta_lin, cot)
    peers = [shifted(pay, "z", d) for d in range(1, zs)]
    vm = pl.BlockSpec(memory_space=pltpu.VMEM)
    grads, bgrad, small = pl.pallas_call(
        after_body,
        in_specs=[pl.BlockSpec(memory_space=pltpu.SMEM)] + [vm] * (zs - 1 + 15),
        out_shape=(
            jax.ShapeDtypeStruct((RIM + length, 4 * DK), BF16),
            jax.ShapeDtypeStruct((length, 1), F32),
            jax.ShapeDtypeStruct((DK + 16, DK), BF16),
        ),
        scratch_shapes=[
            pltpu.VMEM((3, RIM + length, DK), F32),
            pltpu.VMEM((3, RIM + length + 8, DK), F32),
        ],
        name="after",
    )(
        quarter.reshape(1), *peers, proj, up, taps, rate, beta_lin, cot,
        cum, inv, uw, score, mix, back, maps, adds, gives,
    )
    bgrad = bgrad.astype(BF16)

    w_part = lax.dot_general(
        reach, grads, (((0,), (0,)), ((), ())), preferred_element_type=F32
    ).astype(BF16)
    w_sum = lax.psum_scatter(w_part, "z", scatter_dimension=0, tiled=True)

    incoming = lax.ppermute(grads[0:RIM], "z", [(i, i - 1) for i in range(1, zs)])
    ends = (grads[length:].astype(F32) + incoming.astype(F32)).astype(BF16)
    own = jnp.concatenate([grads[RIM:length], ends], axis=0)
    own = jnp.concatenate([own, jnp.pad(bgrad, ((0, 0), (0, DK - 1)))], axis=1)
    sixteen = length // (xs * ys * cs)
    by_core = own.reshape(xs, ys, cs, sixteen, 5 * DK)
    wide_weights = jnp.concatenate(
        [weights, jnp.pad(jnp.transpose(w_strength), ((0, 0), (0, DK - 1)))], axis=1
    )

    def input_part(which):
        part = lax.dynamic_index_in_dim(by_core, which, axis=2, keepdims=False)
        return lax.dot_general(
            part.reshape(length // cs, 5 * DK), wide_weights, (((1,), (1,)), ((), ())),
            preferred_element_type=F32,
        )

    for_other = shifted(input_part(1 - core).astype(BF16), "c", 1)
    pair = (input_part(core) + for_other.astype(F32)).astype(BF16)
    pair = pair.reshape(xs, ys * sixteen, width)
    line = ring_scatter(
        [lax.dynamic_index_in_dim(pair, (head + d) % xs, 0, keepdims=False) for d in range(xs)], "x"
    )
    line = line.astype(BF16).reshape(ys, sixteen, width)
    grad_input = ring_scatter(
        [lax.dynamic_index_in_dim(line, (row + d) % ys, 0, keepdims=False) for d in range(ys)], "y"
    ).astype(BF16)

    beta_part = lax.dot_general(
        bgrad, tokens, (((0,), (0,)), ((), ())), preferred_element_type=F32
    )
    beta_part = beta_part.astype(BF16).reshape(zs * xs, rows_own)
    beta_part = jnp.pad(beta_part, ((0, 0), (0, 2 * DK - rows_own))).reshape(zs, 2 * xs, DK)
    beta_part = jnp.pad(beta_part, ((0, 0), (0, 16 - 2 * xs), (0, 0)))

    def small_for(d):
        rows = lax.dynamic_index_in_dim(beta_part, (quarter + d) % zs, 0, keepdims=False)
        return jnp.concatenate([small, rows], axis=0)

    shared = ordered_sum([small_for(d) for d in range(zs)], "z").astype(BF16)
    common = shared[: DK + 16]
    beta_sum = shared[DK + 16 : DK + 16 + 2 * xs].reshape(xs, 2, DK)

    def final_for(d):
        rows = lax.dynamic_index_in_dim(beta_sum, (head + d) % xs, 0, keepdims=False)
        return jnp.concatenate([common, jnp.pad(rows, ((0, 14), (0, 0)))], axis=0)

    shared = placed(
        [final_for(0)] + [shifted(final_for(d), "x", d) for d in range(1, xs)], "x"
    ).astype(F32)
    beta_rows = shared[:, DK + 16 : DK + 18].reshape(xs, 2 * DK)[:, :rows_own]
    grad_beta = jnp.transpose(beta_rows)
    shared = jnp.transpose(shared[:, : DK + 16], (1, 0, 2)).reshape(DK + 16, xs * DK)
    grad_up = shared[0:DK]
    grad_conv = shared[DK : DK + 3 * CONV].reshape(3, CONV, xs * DK)
    grad_rate = shared[DK + 3 * CONV]

    pieces = lax.all_to_all(w_sum.reshape(xs, rows_own, 4 * DK), "x", 0, 0, tiled=True)

    def wide(kind):
        part = pieces[:, :, kind * DK : (kind + 1) * DK]
        return jnp.transpose(part, (1, 0, 2)).reshape(rows_own, xs * DK).astype(F32)

    down_part = jnp.sum(pieces[:, :, 3 * DK :].astype(F32), axis=0).astype(BF16)
    down_pair = (down_part.astype(F32) + shifted(down_part, "c", 1).astype(F32)).astype(BF16)
    grad_down = ordered_sum([down_pair] * ys, "y")
    return (
        grad_input,
        wide(0),
        wide(1),
        wide(2),
        grad_beta,
        grad_down,
        grad_up,
        grad_conv,
        grad_rate,
    )


def solution(mesh):
    shape = dict(mesh.shape)
    seq, fsdp = shape["seq"], shape["fsdp"]
    xs = 4
    inner = Mesh(mesh.devices.reshape(seq // xs, xs, fsdp // 2, 2), ("z", "x", "y", "c"))
    s, f = ("z", "x"), ("y", "c")
    return jax.shard_map(
        on_device,
        mesh=inner,
        in_specs=(
            P(s, None),
            P(s, f),
            P(s, f),
            P(s, f),
            P(s, f),
            P(s, f),
            P(s, None),
            P(None, f),
            P(None, None, f),
            P(f),
        ),
        out_specs=(
            P(s + f, None),
            P(s, f),
            P(s, f),
            P(s, f),
            P(s, f),
            P(s, None),
            P(None, f),
            P(None, None, f),
            P(f),
        ),
        check_vma=False,
    )
```
